32 devices in a mesh: row: 4 (over z), col: 8 (over y, x, core).
Axes of the slice: x: 2, y: 2, z: 4, core: 2. Of those that a mesh axis runs over, the one named last changes fastest.
Arguments:
- top_in: bfloat16 [8, 96, 1920], P('col'), may hold values from -6 to 6
- bottom_in: bfloat16 [8, 96, 1920], P('col'), may hold values from -6 to 6
- row_tensor: bfloat16 [4, 8, 20, 20, 400], P('row', 'col'), may hold values from -0.3125 to 0.3125
- left_proj: bfloat16 [2, 4, 8, 96, 1920], P(None, 'row', 'col'), may hold values from -0.125 to 0.125
- right_proj: bfloat16 [2, 4, 8, 96, 1920], P(None, 'row', 'col'), may hold values from -0.125 to 0.125
Outputs:
- env: bfloat16 [2, 4, 8, 96, 1920], P(None, 'row', 'col')
The draws below stay inside these ranges and needn't reach their ends.
All inputs are finite; a program needn't handle non-finite values.
Results may differ from the reference program's by a relative error of at most 0.014.
Values may be sent and summed in bfloat16 or wider, within the bound.
A program may use at most 128 MiB of HBM per device.

```python
import jax
import jax.numpy as jnp
from jax import lax

CHI = 96
SECTOR = 32
D2 = 20
COLS = 8
ROWS = 4


def block_scale(own_key, extent, split, least, largest):
    def one(axis_at, blocks):
        heights = jax.random.uniform(jax.random.fold_in(jax.random.fold_in(own_key, 6), axis_at), (blocks,), jnp.float32, least / len(split), largest / len(split))
        return jnp.repeat(jnp.exp(heights), extent[axis_at] // blocks).reshape((-1,) + (1,) * (len(extent) - axis_at - 1))

    factor_of = one(*split[0])
    for cut in split[1:]:
        factor_of = factor_of * one(*cut)
    return factor_of


def centred(key, shape, scale, bound, cuts=(), kind=jnp.bfloat16):
    loudness = block_scale(key, shape, cuts, -0.22, 0.18) if cuts else 1.0
    entries = jax.random.normal(key, shape, jnp.float32) * scale * loudness
    return jnp.minimum(jnp.maximum(entries, -bound), bound).astype(kind)


def setup_inputs(seed: int = 0) -> dict:
    key_of = jax.random.split(jax.random.key(seed), 6)
    return {
        "top_in": centred(key_of[0], (COLS, CHI, D2 * CHI), 1.0, 6.0, ((0, 8),)),
        "bottom_in": centred(key_of[1], (COLS, CHI, D2 * CHI), 1.0, 6.0, ((0, 8),)),
        "row_tensor": centred(key_of[2], (ROWS, COLS, D2, D2, D2 * D2), (D2 * D2) ** -0.5, 0.3125, ((0, 4), (1, 8))),
        "left_proj": centred(key_of[3], (2, ROWS, COLS, CHI, D2 * CHI), (CHI * D2) ** -0.5, 0.125, ((1, 4), (2, 8))),
        "right_proj": centred(key_of[4], (2, ROWS, COLS, CHI, D2 * CHI), (CHI * D2) ** -0.5, 0.125, ((1, 4), (2, 8))),
    }


epsilon = 1e-06

def absorb_column(boundary, row_site, left_proj, right_proj):
    blocks = CHI // SECTOR
    left_blocks = jnp.moveaxis(left_proj.reshape(CHI, D2, blocks, SECTOR), 2, 0)
    boundary_wide = boundary.astype(jnp.float32)
    site_wide = row_site.astype(jnp.float32)
    right_wide = right_proj.astype(jnp.float32)

    def one_block(block_proj):
        first_part = jnp.einsum('lLa,lur->aLur', block_proj.astype(jnp.float32), boundary_wide).astype(jnp.bfloat16)
        second_part = jnp.einsum('aLur,LuRd->Rdar', first_part.astype(jnp.float32), site_wide).astype(jnp.bfloat16)
        return jnp.einsum('Rdar,rRb->adb', second_part.astype(jnp.float32), right_wide)
    grown_site = lax.map(one_block, left_blocks).reshape(CHI, D2, CHI)
    factor = lax.rsqrt(jnp.mean(grown_site * grown_site) + epsilon)
    return (grown_site * factor).astype(jnp.bfloat16)

def absorb_row(boundary, row_sites, left_proj, right_proj):

    def one_column(items):
        return absorb_column(items[0], items[1], items[2], items[3])
    return lax.map(one_column, (boundary, row_sites, left_proj, right_proj))

def reference(top_in, bottom_in, row_tensor, left_proj, right_proj):
    down_tensor = row_tensor.reshape(ROWS, COLS, D2, D2, D2, D2)
    up_tensor = jnp.transpose(down_tensor, (0, 1, 2, 5, 4, 3))
    left_full = left_proj.reshape(2, ROWS, COLS, CHI, D2, CHI)
    right_full = right_proj.reshape(2, ROWS, COLS, CHI, D2, CHI)
    top_results = [None] * ROWS
    bottom_results = [None] * ROWS
    current = top_in.reshape(COLS, CHI, D2, CHI)
    for lattice_row in range(ROWS):
        current = absorb_row(current, down_tensor[lattice_row], jnp.roll(left_full[0, lattice_row], 1, axis=0), right_full[0, lattice_row])
        top_results[lattice_row] = current
    current = bottom_in.reshape(COLS, CHI, D2, CHI)
    for lattice_row in range(ROWS - 1, -1, -1):
        current = absorb_row(current, up_tensor[lattice_row], jnp.roll(left_full[1, lattice_row], 1, axis=0), right_full[1, lattice_row])
        bottom_results[lattice_row] = current
    stacked = jnp.stack([jnp.stack(top_results), jnp.stack(bottom_results)])
    return stacked.reshape(2, ROWS, COLS, CHI, D2 * CHI)
```

```python
import functools

import jax
import jax.numpy as jnp
from jax import lax
from jax.experimental import pallas as pl
from jax.experimental.pallas import tpu as pltpu
from jax.sharding import PartitionSpec as P

epsilon = 1e-06
LANES = 128
WIDE = 64
UNIT = 32
SUB = 8
TALL = 16
GROUP = 3
BF = jnp.bfloat16
F32 = jnp.float32


def round_up(value, unit):
    return -(-value // unit) * unit


def lane_roll(value, amount):
    return pltpu.roll(value, amount, 1) if amount else value


def sweep_kernel(rows, cols, chi, pair, top_hbm, bottom_hbm, tensor_hbm, left_hbm, right_hbm, env_ref,
                 tensor, right, held, leftraw, tall, turned, pieces, site, left_tall, left_rows, right_rows,
                 wide, first, spread, out, grown, total, stage, landed, scaling,
                 local_sem, left_send, left_recv, send_sem, recv_sem):
    row = lax.axis_index("row")
    col = lax.axis_index("col")
    half = chi // 2
    blocks = half // SUB
    groups = blocks // GROUP
    low_legs = TALL
    high_legs = pair - TALL
    block_rows = SUB * pair
    tail_at = SUB * TALL
    padded = round_up(pair, SUB)
    bond = chi * 4
    chunks = pair // 4
    begin = jnp.where(row < rows // 2, 0, 1)

    def copy_in(source, target, at):
        return pltpu.make_async_copy(source, target, local_sem.at[at])

    copy_in(tensor_hbm, tensor, 0).start()
    copy_in(right_hbm, right, 1).start()

    @pl.when(row < rows // 2)
    def _():
        copy_in(top_hbm, held, 2).start()

    @pl.when(row >= rows // 2)
    def _():
        copy_in(bottom_hbm, held, 2).start()

    barrier = pltpu.get_barrier_semaphore()
    for step in (1, cols - 1):
        pl.semaphore_signal(barrier, inc=1, device_id={"col": lax.rem(col + step, cols)}, device_id_type=pl.DeviceIdType.MESH)

    @pl.when(row > 0)
    def _():
        pl.semaphore_signal(barrier, inc=1, device_id={"row": row - 1}, device_id_type=pl.DeviceIdType.MESH)

    @pl.when(row < rows - 1)
    def _():
        pl.semaphore_signal(barrier, inc=1, device_id={"row": row + 1}, device_id_type=pl.DeviceIdType.MESH)

    pl.semaphore_wait(barrier, 2 + jnp.where(row > 0, 1, 0) + jnp.where(row < rows - 1, 1, 0))

    def left_copy(which, chunk):
        return pltpu.make_async_remote_copy(
            src_ref=left_hbm.at[which, :, pl.ds(chunk * bond, bond)],
            dst_ref=leftraw.at[which, :, pl.ds(chunk * bond, bond)],
            send_sem=left_send.at[which, chunk],
            recv_sem=left_recv.at[which, chunk],
            device_id={"col": lax.rem(col + 1, cols)},
            device_id_type=pl.DeviceIdType.MESH,
        )

    for which in (begin, 1 - begin):
        for chunk in range(chunks):
            left_copy(which, chunk).start()

    wide[...] = jnp.zeros_like(wide)
    right_rows[...] = jnp.zeros_like(right_rows)
    left_tall[...] = jnp.zeros_like(left_tall)
    tall[...] = jnp.zeros_like(tall)
    pieces[...] = jnp.zeros_like(pieces)

    lane_unit = lax.broadcasted_iota(jnp.int32, (SUB, LANES), 1) // UNIT
    low = lane_unit < 2
    low_tall = (lax.broadcasted_iota(jnp.int32, (TALL, LANES), 1) // UNIT) < 2
    sub = lax.broadcasted_iota(jnp.int32, (SUB, LANES), 0) < SUB // 2
    diag = low == sub
    tall_unit = lax.broadcasted_iota(jnp.int32, (TALL, LANES), 1) // UNIT

    def swap_lanes(value):
        return pltpu.roll(value, WIDE, 1)

    def swap_sub(value):
        return pltpu.roll(value, SUB // 2, 0)

    def order(index):
        split = pair * TALL
        later = index - split
        big = jnp.where(index < split, index // TALL, later // high_legs)
        small = jnp.where(index < split, index % TALL, TALL + later % high_legs)
        return big, small

    def permuted(value):
        return jnp.concatenate(
            [value[s * half + k * SUB:s * half + (k + 1) * SUB] for k in range(blocks) for s in range(2)], axis=0
        )

    def prepare(which):
        slabs, slab, _ = tall.shape
        count = pair * pair
        for leg in range(pair):
            plane = tensor[leg].astype(F32)
            for part in range(slabs):
                lanes = min(LANES, count - part * LANES)
                tall[part, pl.ds(leg, pair, stride=padded), :lanes] = plane[:, part * LANES:part * LANES + lanes]
        for part in range(slabs):
            for other in range(slabs):
                turned[other, part * LANES:(part + 1) * LANES, :] = tall[part, other * LANES:(other + 1) * LANES, :].T
        big, small = order(lax.broadcasted_iota(jnp.int32, (1, count), 1))
        pick_lanes = (lax.broadcasted_iota(jnp.int32, (slab, count), 0) == big * padded + small).astype(F32).astype(BF)
        big, small = order(lax.broadcasted_iota(jnp.int32, (count, 1), 0))

        def finish(source, wanted):
            pick_rows = (lax.broadcasted_iota(jnp.int32, (count, slab), 1) == wanted).astype(F32).astype(BF)
            ordered = jnp.dot(pick_rows, source.astype(BF), preferred_element_type=F32).astype(BF)
            site[which] = jnp.dot(ordered, pick_lanes, preferred_element_type=F32).astype(BF)

        @pl.when(which == 0)
        def _():
            finish(jnp.concatenate([turned[part] for part in range(slabs)], axis=1), big * pair + small)

        @pl.when(which == 1)
        def _():
            for near in range(pair):
                lines = jnp.concatenate([turned[part, pl.ds(near, pair, stride=pair), :] for part in range(slabs)], axis=1)
                for far in range(pair):
                    pieces[far * padded:far * padded + pair, near * padded:(near + 1) * padded] = (
                        lines[:, far * padded:(far + 1) * padded]
                    )
            finish(pieces[...], small * padded + big)

        for leg in range(pair):
            base = (leg // 2) * 3 * LANES
            block = right[which, :, leg * chi:(leg + 1) * chi]
            for s in range(2):
                at = base + (leg % 2) * LANES + s * WIDE
                right_rows[which, at:at + WIDE, s * LANES:s * LANES + chi] = block[:WIDE]
                at = base + 2 * LANES + (leg % 2) * WIDE + s * UNIT
                right_rows[which, at:at + UNIT, s * LANES:s * LANES + chi] = block[WIDE:]

    def prepare_left(which):
        for leg in range(pair):
            if leg % 4 == 0:
                left_copy(which, leg // 4).wait_recv()
            block = permuted(leftraw[which, :, leg * chi:(leg + 1) * chi].astype(F32)).T
            for k in range(blocks):
                for s in range(2):
                    piece = block[s * half + k * SUB:s * half + (k + 1) * SUB]
                    if leg < TALL:
                        place = pl.ds(k * block_rows + leg, SUB, stride=TALL)
                    else:
                        place = pl.ds(k * block_rows + tail_at + leg - TALL, SUB, stride=high_legs)
                    left_tall[s, place, :chi] = piece
        for s in range(2):
            left_rows[which, :, s * LANES:(s + 1) * LANES] = left_tall[s].astype(BF)

    def copy_of(which, block):
        at = pl.multiple_of(block * 2 * SUB, 2 * SUB)
        return pltpu.make_async_remote_copy(
            src_ref=stage.at[pl.ds(at, 2 * SUB)],
            dst_ref=landed.at[which, pl.ds(at, 2 * SUB)],
            send_sem=send_sem.at[block],
            recv_sem=recv_sem.at[which, block],
            device_id={"row": jnp.where(which == 0, row + 1, row - 1)},
            device_id_type=pl.DeviceIdType.MESH,
        )

    def inverse_norm(square_sum):
        return lax.rsqrt(jnp.full((1, 1), jnp.sum(square_sum) / (chi * pair * chi) + epsilon, F32))

    def unpack(which, block):
        at = pl.multiple_of(block * 2 * SUB, 2 * SUB)
        squares = jnp.zeros((SUB, LANES), F32)
        for quad in range(pair // 4):
            tiles = [
                landed[which, pl.ds(at, 2 * SUB), (3 * quad + t) * LANES:(3 * quad + t + 1) * LANES].astype(F32)
                for t in range(3)
            ]
            for tile in tiles:
                squares += jnp.sum((tile * tile).reshape(2, SUB, LANES), axis=0)

            def unit(leg, part, place):
                source, position = divmod(leg * 3 + part, 4)
                return lane_roll(tiles[source], (place - position) % 4 * UNIT)

            def build(parts, s):
                value = jnp.zeros((TALL, LANES), F32)
                for leg, part, place in parts:
                    value = jnp.where(tall_unit == place, unit(leg, part, place), value)
                return value.astype(BF)

            for s in range(2):
                for duo in range(2):
                    base = (2 * quad + duo) * 3 * LANES
                    for v in range(2):
                        leg = 2 * duo + v
                        wide[pl.ds(pl.multiple_of(s * LANES + at, TALL), TALL), base + v * LANES:base + (v + 1) * LANES] = (
                            build([(leg, 0, 2 * s), (leg, 1, 2 * s + 1)], s)
                        )
                    wide[pl.ds(pl.multiple_of(s * LANES + at, TALL), TALL), base + 2 * LANES:base + 3 * LANES] = (
                        build([(2 * duo, 2, s), (2 * duo + 1, 2, 2 + s)], s)
                    )
        return squares

    def mix(tile):
        p, q, x = tile[:, :LANES], tile[:, LANES:2 * LANES], tile[:, 2 * LANES:]
        return (
            jnp.where(sub, p, swap_sub(q)),
            jnp.where(sub, swap_sub(p), q),
            jnp.where(diag, x, swap_lanes(swap_sub(x))),
        )

    def cross(upper, lower):
        x, y = upper[:, 2 * LANES:], lower[:, 2 * LANES:]
        return jnp.where(low_tall, x, swap_lanes(y)), jnp.where(low_tall, swap_lanes(x), y)

    def absorb(which, sends, first_group, last_group):
        total[...] = jnp.zeros_like(total)
        split = pair * TALL

        def contract_left(block):
            left_here = left_rows[which, pl.ds(pl.multiple_of(block * block_rows, block_rows), block_rows), :]
            for quad in range(pair // 4):
                part = jnp.dot(left_here, wide[:, quad * 6 * LANES:(quad + 1) * 6 * LANES], preferred_element_type=F32)
                halves = [part[:, :3 * LANES], part[:, 3 * LANES:]]
                for duo in range(2):
                    at = (2 * quad + duo) * 2 * TALL
                    for two in range(SUB // 2):
                        upper = halves[duo][2 * two * TALL:(2 * two + 1) * TALL]
                        lower = halves[duo][(2 * two + 1) * TALL:(2 * two + 2) * TALL]
                        pairs = (
                            (upper[:, :LANES], upper[:, LANES:2 * LANES]),
                            (lower[:, :LANES], lower[:, LANES:2 * LANES]),
                            cross(upper, lower),
                        )
                        for t in range(3):
                            lanes = slice((3 * two + t) * LANES, (3 * two + t + 1) * LANES)
                            first[at:at + TALL, lanes] = pairs[t][0].astype(BF)
                            first[at + TALL:at + 2 * TALL, lanes] = pairs[t][1].astype(BF)
                for two in range(SUB // 2):
                    mixed = [mix(halves[duo][tail_at + two * SUB:tail_at + (two + 1) * SUB]) for duo in range(2)]
                    for t in range(3):
                        first[split + quad * TALL:split + (quad + 1) * TALL, (3 * two + t) * LANES:(3 * two + t + 1) * LANES] = (
                            jnp.concatenate([mixed[0][t], mixed[1][t]], axis=0).astype(BF)
                        )

        def contract_site():
            for four in range(SUB // 4):
                part = jnp.dot(site[which], first[:, four * 6 * LANES:(four + 1) * 6 * LANES], preferred_element_type=F32)
                halves = [part[:, :3 * LANES], part[:, 3 * LANES:]]
                for duo in range(pair // 2):
                    for two in range(2):
                        at = (4 * four + 2 * two) * TALL
                        upper = halves[two][2 * duo * TALL:(2 * duo + 1) * TALL]
                        lower = halves[two][(2 * duo + 1) * TALL:(2 * duo + 2) * TALL]
                        pairs = (
                            (upper[:, :LANES], upper[:, LANES:2 * LANES]),
                            (lower[:, :LANES], lower[:, LANES:2 * LANES]),
                            cross(upper, lower),
                        )
                        for t in range(3):
                            lanes = slice((3 * duo + t) * LANES, (3 * duo + t + 1) * LANES)
                            spread[at:at + TALL, lanes] = pairs[t][0].astype(BF)
                            spread[at + TALL:at + 2 * TALL, lanes] = pairs[t][1].astype(BF)
                    mixed = [mix(halves[two][split + duo * SUB:split + (duo + 1) * SUB]) for two in range(2)]
                    for t in range(3):
                        spread[tail_at + four * TALL:tail_at + (four + 1) * TALL, (3 * duo + t) * LANES:(3 * duo + t + 1) * LANES] = (
                            jnp.concatenate([mixed[0][t], mixed[1][t]], axis=0).astype(BF)
                        )

        def contract_right(block):
            done = jnp.dot(spread[...], right_rows[which], preferred_element_type=F32) * scaling[...]
            total[...] += jnp.sum((done * done).reshape(-1, SUB, 2 * LANES), axis=0)
            for s in range(2):
                out[s] = done[:, s * LANES:(s + 1) * LANES]
            at = pl.multiple_of(block * 2 * SUB, 2 * SUB)
            for quad in range(pair // 4):
                lines = []
                for leg in range(4 * quad, 4 * quad + 4):
                    if leg < TALL:
                        place = pl.ds(leg, SUB, stride=TALL)
                    else:
                        place = pl.ds(tail_at + leg - TALL, SUB, stride=high_legs)
                    lines.append([out[s, place, :] for s in range(2)])
                both = []
                for s in range(2):
                    moved = [
                        lane_roll(lines[leg][s], (-leg) % 4 * UNIT) for leg in range(4)
                    ]
                    both.append([
                        jnp.where(lane_unit < 3 - t, moved[t], moved[t + 1]) for t in range(3)
                    ])
                for t in range(3):
                    lanes = slice((3 * quad + t) * LANES, (3 * quad + t + 1) * LANES)
                    for s in range(2):
                        grown[pl.ds(pl.multiple_of(s * half + block * SUB, SUB), SUB), lanes] = both[s][t]
                    stage[pl.ds(at, 2 * SUB), lanes] = jnp.concatenate([both[0][t], both[1][t]], axis=0).astype(BF)

            @pl.when(sends)
            def _():
                copy_of(which, block).start()

        contract_left(first_group * GROUP)

        def one_group(group, carry):
            for place in range(GROUP):
                block = group * GROUP + place
                contract_site()
                if place < GROUP - 1:
                    contract_left(block + 1)
                else:
                    @pl.when(group < last_group - 1)
                    def _():
                        contract_left(block + 1)
                contract_right(block)
            return carry

        lax.fori_loop(first_group, last_group, one_group, 0)
        factor = inverse_norm(total[...])
        env_ref[which] = (grown[...] * factor).astype(BF)

    def one_turn(turn, carry):
        which = jnp.where(row == turn, 0, 1)
        active = (row == turn) | (row == rows - 1 - turn)
        sends = turn < rows - 1
        early = jnp.where((row == 0) | (row == rows - 1), 1, 2)

        def one_prepare(step, carry):
            mine = jnp.where(step == 0, begin, 1 - begin)
            prepare(mine)
            prepare_left(mine)
            return carry

        @pl.when(turn == 0)
        def _():
            copy_in(tensor_hbm, tensor, 0).wait()
            copy_in(right_hbm, right, 1).wait()
            copy_in(top_hbm, held, 2).wait()

        @pl.when(active & (turn == 0))
        def _():
            for lanes in range(0, pair * chi, LANES):
                landed[which, :, lanes:lanes + LANES] = permuted(held[:, lanes:lanes + LANES].astype(F32)).astype(BF)

        lax.fori_loop(
            jnp.where(turn == 0, 0, jnp.where(turn == 1, early, 2)), jnp.where(turn == 0, early, 2), one_prepare, 0
        )

        @pl.when(active)
        def _():
            def one_unpack(block, squares):
                @pl.when(turn > 0)
                def _():
                    copy_of(which, block).wait_recv()

                return squares + unpack(which, block)

            squares = lax.fori_loop(0, blocks, one_unpack, jnp.zeros((SUB, LANES), F32))
            norm = jnp.where(turn > 0, inverse_norm(squares), jnp.ones((1, 1), F32))
            scaling[...] = jnp.broadcast_to(norm, scaling.shape)
            absorb(which, sends, 0, groups)

        @pl.when(active & sends)
        def _():
            for block in range(blocks):
                copy_of(which, block).wait_send()

        return carry

    lax.fori_loop(0, rows, one_turn, 0)
    for which in range(2):
        for chunk in range(chunks):
            left_copy(which, chunk).wait_send()


def sweep(rows, cols, top, bottom, tensor, left, right, chi, pair):
    slab = round_up(pair * round_up(pair, SUB), LANES)
    count = pair * pair
    half = chi // 2
    blocks = half // SUB
    lanes = pair // 2 * 3 * LANES
    return pl.pallas_call(
        functools.partial(sweep_kernel, rows, cols, chi, pair),
        out_shape=jax.ShapeDtypeStruct((2,) + top.shape, top.dtype),
        in_specs=[pl.BlockSpec(memory_space=pl.ANY)] * 5,
        out_specs=pl.BlockSpec(memory_space=pltpu.VMEM),
        scratch_shapes=[
            pltpu.VMEM(tensor.shape, BF),
            pltpu.VMEM(right.shape, BF),
            pltpu.VMEM(top.shape, BF),
            pltpu.VMEM(left.shape, BF),
            pltpu.VMEM((slab // LANES, slab, LANES), F32),
            pltpu.VMEM((slab // LANES, slab, LANES), F32),
            pltpu.VMEM((slab, slab), F32),
            pltpu.VMEM((2, count, count), BF),
            pltpu.VMEM((2, half * pair, LANES), F32),
            pltpu.VMEM((2, half * pair, 2 * LANES), BF),
            pltpu.VMEM((2, lanes, 2 * LANES), BF),
            pltpu.VMEM((2 * LANES, lanes), BF),
            pltpu.VMEM((count, SUB // 2 * 3 * LANES), BF),
            pltpu.VMEM((SUB * pair, lanes), BF),
            pltpu.VMEM((2, SUB * pair, LANES), F32),
            pltpu.VMEM(top.shape, F32),
            pltpu.VMEM((SUB, 2 * LANES), F32),
            pltpu.VMEM(top.shape, BF),
            pltpu.VMEM((2,) + top.shape, BF),
            pltpu.VMEM((1, 2 * LANES), F32),
            pltpu.SemaphoreType.DMA((3,)),
            pltpu.SemaphoreType.DMA((2, pair // 4)),
            pltpu.SemaphoreType.DMA((2, pair // 4)),
            pltpu.SemaphoreType.DMA((blocks,)),
            pltpu.SemaphoreType.DMA((2, blocks)),
        ],
        compiler_params=pltpu.CompilerParams(collective_id=0, has_side_effects=True, vmem_limit_bytes=40 * 1024 * 1024),
        name="sweep",
    )(top, bottom, tensor, left, right)


def local(top_in, bottom_in, row_tensor, left_proj, right_proj):
    chi = top_in.shape[1]
    pair = row_tensor.shape[2]
    env = sweep(
        lax.axis_size("row"), lax.axis_size("col"), top_in[0], bottom_in[0], row_tensor[0, 0],
        left_proj[:, 0, 0], right_proj[:, 0, 0], chi, pair,
    )
    return env[:, None, None]


def solution(mesh):
    return jax.shard_map(
        local,
        mesh=mesh,
        in_specs=(
            P("col", None, None),
            P("col", None, None),
            P("row", "col", None, None, None),
            P(None, "row", "col", None, None),
            P(None, "row", "col", None, None),
        ),
        out_specs=P(None, "row", "col", None, None),
        check_vma=False,
    )
```

```python
import functools

import jax
import jax.numpy as jnp
from jax import lax
from jax.experimental import pallas as pl
from jax.experimental.pallas import tpu as pltpu
from jax.sharding import PartitionSpec as P

epsilon = 1e-06
LANES = 128
WIDE = 64
UNIT = 32
SUB = 8
TALL = 16
GROUP = 3
FAR = 2
BF = jnp.bfloat16
F32 = jnp.float32


def round_up(value, unit):
    return -(-value // unit) * unit


def lane_roll(value, amount):
    return pltpu.roll(value, amount, 1) if amount else value


def sweep_kernel(rows, cols, chi, pair, top_hbm, bottom_hbm, tensor_hbm, left_hbm, right_hbm, env_ref,
                 tensor, right, held, leftraw, tall, turned, pieces, site, left_tall, left_rows, right_rows,
                 wide, first, spread, out, grown, total, landed, scaling, right_far,
                 local_sem, left_send, left_recv, send_sem, recv_sem, far_send, far_recv):
    row = lax.axis_index("row")
    col = lax.axis_index("col")
    half = chi // 2
    blocks = half // SUB
    groups = blocks // GROUP
    low_legs = TALL
    high_legs = pair - TALL
    block_rows = SUB * pair
    tail_at = SUB * TALL
    padded = round_up(pair, SUB)
    bond = chi * 4
    chunks = pair // 4
    begin = jnp.where(row < rows // 2, 0, 1)
    split = rows > 2

    def copy_in(source, target, at):
        return pltpu.make_async_copy(source, target, local_sem.at[at])

    copy_in(tensor_hbm, tensor, 0).start()
    copy_in(right_hbm, right, 1).start()

    @pl.when(row < rows // 2)
    def _():
        copy_in(top_hbm, held, 2).start()

    @pl.when(row >= rows // 2)
    def _():
        copy_in(bottom_hbm, held, 2).start()

    barrier = pltpu.get_barrier_semaphore()
    for step in (1, cols - 1):
        pl.semaphore_signal(barrier, inc=1, device_id={"col": lax.rem(col + step, cols)}, device_id_type=pl.DeviceIdType.MESH)

    @pl.when(row > 0)
    def _():
        pl.semaphore_signal(barrier, inc=1, device_id={"row": row - 1}, device_id_type=pl.DeviceIdType.MESH)

    @pl.when(row < rows - 1)
    def _():
        pl.semaphore_signal(barrier, inc=1, device_id={"row": row + 1}, device_id_type=pl.DeviceIdType.MESH)

    pl.semaphore_wait(barrier, 2 + jnp.where(row > 0, 1, 0) + jnp.where(row < rows - 1, 1, 0))

    def left_copy(which, chunk):
        return pltpu.make_async_remote_copy(
            src_ref=left_hbm.at[which, :, pl.ds(chunk * bond, bond)],
            dst_ref=leftraw.at[which, :, pl.ds(chunk * bond, bond)],
            send_sem=left_send.at[which, chunk],
            recv_sem=left_recv.at[which, chunk],
            device_id={"col": lax.rem(col + 1, cols)},
            device_id_type=pl.DeviceIdType.MESH,
        )

    outer = (row == 0) | (row == rows - 1)
    helping = (row == 1) | (row == rows - 2)
    inward = jnp.where(row < rows // 2, row + 1, row - 1)
    cut = blocks // 2 * block_rows

    def far_copy(item):
        mine = 1 - begin
        source, target = (
            (right_hbm.at[mine], right_far),
            (site.at[mine], site.at[FAR]),
            (left_rows.at[mine, pl.ds(cut, cut)], left_rows.at[FAR, pl.ds(cut, cut)]),
        )[item]
        return pltpu.make_async_remote_copy(
            src_ref=source,
            dst_ref=target,
            send_sem=far_send.at[item],
            recv_sem=far_recv.at[item],
            device_id={"row": inward},
            device_id_type=pl.DeviceIdType.MESH,
        )

    for chunk in range(chunks):
        left_copy(begin, chunk).start()

    if split:
        @pl.when(outer)
        def _():
            far_copy(0).start()

    for chunk in range(chunks):
        left_copy(1 - begin, chunk).start()

    wide[...] = jnp.zeros_like(wide)
    right_rows[...] = jnp.zeros_like(right_rows)
    left_tall[...] = jnp.zeros_like(left_tall)
    tall[...] = jnp.zeros_like(tall)
    pieces[...] = jnp.zeros_like(pieces)

    lane_unit = lax.broadcasted_iota(jnp.int32, (SUB, LANES), 1) // UNIT
    low = lane_unit < 2
    low_tall = (lax.broadcasted_iota(jnp.int32, (TALL, LANES), 1) // UNIT) < 2
    sub = lax.broadcasted_iota(jnp.int32, (SUB, LANES), 0) < SUB // 2
    diag = low == sub
    tall_unit = lax.broadcasted_iota(jnp.int32, (TALL, LANES), 1) // UNIT

    def swap_lanes(value):
        return pltpu.roll(value, WIDE, 1)

    def swap_sub(value):
        return pltpu.roll(value, SUB // 2, 0)

    def order(index):
        split = pair * TALL
        later = index - split
        big = jnp.where(index < split, index // TALL, later // high_legs)
        small = jnp.where(index < split, index % TALL, TALL + later % high_legs)
        return big, small

    def permuted(value):
        return jnp.concatenate(
            [value[s * half + k * SUB:s * half + (k + 1) * SUB] for k in range(blocks) for s in range(2)], axis=0
        )

    def lay_right(slot, load):
        for leg in range(pair):
            base = (leg // 2) * 3 * LANES
            block = load(slice(leg * chi, (leg + 1) * chi))
            for s in range(2):
                at = base + (leg % 2) * LANES + s * WIDE
                right_rows[slot, at:at + WIDE, s * LANES:s * LANES + chi] = block[:WIDE]
                at = base + 2 * LANES + (leg % 2) * WIDE + s * UNIT
                right_rows[slot, at:at + UNIT, s * LANES:s * LANES + chi] = block[WIDE:]

    def prepare(which):
        slabs, slab, _ = tall.shape
        count = pair * pair
        for leg in range(pair):
            plane = tensor[leg].astype(F32)
            for part in range(slabs):
                lanes = min(LANES, count - part * LANES)
                tall[part, pl.ds(leg, pair, stride=padded), :lanes] = plane[:, part * LANES:part * LANES + lanes]
        for part in range(slabs):
            for other in range(slabs):
                turned[other, part * LANES:(part + 1) * LANES, :] = tall[part, other * LANES:(other + 1) * LANES, :].T
        big, small = order(lax.broadcasted_iota(jnp.int32, (1, count), 1))
        pick_lanes = (lax.broadcasted_iota(jnp.int32, (slab, count), 0) == big * padded + small).astype(F32).astype(BF)
        big, small = order(lax.broadcasted_iota(jnp.int32, (count, 1), 0))

        def finish(source, wanted):
            pick_rows = (lax.broadcasted_iota(jnp.int32, (count, slab), 1) == wanted).astype(F32).astype(BF)
            ordered = jnp.dot(pick_rows, source.astype(BF), preferred_element_type=F32).astype(BF)
            site[which] = jnp.dot(ordered, pick_lanes, preferred_element_type=F32).astype(BF)

        @pl.when(which == 0)
        def _():
            finish(jnp.concatenate([turned[part] for part in range(slabs)], axis=1), big * pair + small)

        @pl.when(which == 1)
        def _():
            for near in range(pair):
                lines = jnp.concatenate([turned[part, pl.ds(near, pair, stride=pair), :] for part in range(slabs)], axis=1)
                for far in range(pair):
                    pieces[far * padded:far * padded + pair, near * padded:(near + 1) * padded] = (
                        lines[:, far * padded:(far + 1) * padded]
                    )
            finish(pieces[...], small * padded + big)

        lay_right(which, lambda lanes: right[which, :, lanes])

    def prepare_left(which):
        for leg in range(pair):
            if leg % 4 == 0:
                left_copy(which, leg // 4).wait_recv()
            block = permuted(leftraw[which, :, leg * chi:(leg + 1) * chi].astype(F32)).T
            for k in range(blocks):
                for s in range(2):
                    piece = block[s * half + k * SUB:s * half + (k + 1) * SUB]
                    if leg < TALL:
                        place = pl.ds(k * block_rows + leg, SUB, stride=TALL)
                    else:
                        place = pl.ds(k * block_rows + tail_at + leg - TALL, SUB, stride=high_legs)
                    left_tall[s, place, :chi] = piece
        for s in range(2):
            left_rows[which, :, s * LANES:(s + 1) * LANES] = left_tall[s].astype(BF)

    def copy_of(which, block, place=None):
        at = pl.multiple_of(block * 2 * SUB, 2 * SUB)
        return pltpu.make_async_remote_copy(
            src_ref=landed.at[FAR, pl.ds(at, 2 * SUB)],
            dst_ref=landed.at[which if place is None else place, pl.ds(at, 2 * SUB)],
            send_sem=send_sem.at[block],
            recv_sem=recv_sem.at[which if place is None else place, block],
            device_id={"row": jnp.where(which == 0, row + 1, row - 1)},
            device_id_type=pl.DeviceIdType.MESH,
        )

    def inverse_norm(square_sum):
        return lax.rsqrt(jnp.full((1, 1), jnp.sum(square_sum) / (chi * pair * chi) + epsilon, F32))

    def unpack(source_at, block):
        at = pl.multiple_of(block * 2 * SUB, 2 * SUB)
        squares = jnp.zeros((SUB, LANES), F32)
        for quad in range(pair // 4):
            tiles = [
                landed[source_at, pl.ds(at, 2 * SUB), (3 * quad + t) * LANES:(3 * quad + t + 1) * LANES].astype(F32)
                for t in range(3)
            ]
            for tile in tiles:
                squares += jnp.sum((tile * tile).reshape(2, SUB, LANES), axis=0)

            def unit(leg, part, place):
                source, position = divmod(leg * 3 + part, 4)
                return lane_roll(tiles[source], (place - position) % 4 * UNIT)

            def build(parts, s):
                value = jnp.zeros((TALL, LANES), F32)
                for leg, part, place in parts:
                    value = jnp.where(tall_unit == place, unit(leg, part, place), value)
                return value.astype(BF)

            for s in range(2):
                for duo in range(2):
                    base = (2 * quad + duo) * 3 * LANES
                    for v in range(2):
                        leg = 2 * duo + v
                        wide[pl.ds(pl.multiple_of(s * LANES + at, TALL), TALL), base + v * LANES:base + (v + 1) * LANES] = (
                            build([(leg, 0, 2 * s), (leg, 1, 2 * s + 1)], s)
                        )
                    wide[pl.ds(pl.multiple_of(s * LANES + at, TALL), TALL), base + 2 * LANES:base + 3 * LANES] = (
                        build([(2 * duo, 2, s), (2 * duo + 1, 2, 2 + s)], s)
                    )
        return squares

    def mix(tile):
        p, q, x = tile[:, :LANES], tile[:, LANES:2 * LANES], tile[:, 2 * LANES:]
        return (
            jnp.where(sub, p, swap_sub(q)),
            jnp.where(sub, swap_sub(p), q),
            jnp.where(diag, x, swap_lanes(swap_sub(x))),
        )

    def cross(upper, lower):
        x, y = upper[:, 2 * LANES:], lower[:, 2 * LANES:]
        return jnp.where(low_tall, x, swap_lanes(y)), jnp.where(low_tall, swap_lanes(x), y)

    def absorb(which, slot, place, sends, first_group, last_group):
        total[...] = jnp.zeros_like(total)
        split = pair * TALL

        def contract_left(block):
            left_here = left_rows[slot, pl.ds(pl.multiple_of(block * block_rows, block_rows), block_rows), :]
            for quad in range(pair // 4):
                part = jnp.dot(left_here, wide[:, quad * 6 * LANES:(quad + 1) * 6 * LANES], preferred_element_type=F32)
                halves = [part[:, :3 * LANES], part[:, 3 * LANES:]]
                for duo in range(2):
                    at = (2 * quad + duo) * 2 * TALL
                    for two in range(SUB // 2):
                        upper = halves[duo][2 * two * TALL:(2 * two + 1) * TALL]
                        lower = halves[duo][(2 * two + 1) * TALL:(2 * two + 2) * TALL]
                        pairs = (
                            (upper[:, :LANES], upper[:, LANES:2 * LANES]),
                            (lower[:, :LANES], lower[:, LANES:2 * LANES]),
                            cross(upper, lower),
                        )
                        for t in range(3):
                            lanes = slice((3 * two + t) * LANES, (3 * two + t + 1) * LANES)
                            first[at:at + TALL, lanes] = pairs[t][0].astype(BF)
                            first[at + TALL:at + 2 * TALL, lanes] = pairs[t][1].astype(BF)
                for two in range(SUB // 2):
                    mixed = [mix(halves[duo][tail_at + two * SUB:tail_at + (two + 1) * SUB]) for duo in range(2)]
                    for t in range(3):
                        first[split + quad * TALL:split + (quad + 1) * TALL, (3 * two + t) * LANES:(3 * two + t + 1) * LANES] = (
                            jnp.concatenate([mixed[0][t], mixed[1][t]], axis=0).astype(BF)
                        )

        def contract_site():
            for four in range(SUB // 4):
                part = jnp.dot(site[slot], first[:, four * 6 * LANES:(four + 1) * 6 * LANES], preferred_element_type=F32)
                halves = [part[:, :3 * LANES], part[:, 3 * LANES:]]
                for duo in range(pair // 2):
                    for two in range(2):
                        at = (4 * four + 2 * two) * TALL
                        upper = halves[two][2 * duo * TALL:(2 * duo + 1) * TALL]
                        lower = halves[two][(2 * duo + 1) * TALL:(2 * duo + 2) * TALL]
                        pairs = (
                            (upper[:, :LANES], upper[:, LANES:2 * LANES]),
                            (lower[:, :LANES], lower[:, LANES:2 * LANES]),
                            cross(upper, lower),
                        )
                        for t in range(3):
                            lanes = slice((3 * duo + t) * LANES, (3 * duo + t + 1) * LANES)
                            spread[at:at + TALL, lanes] = pairs[t][0].astype(BF)
                            spread[at + TALL:at + 2 * TALL, lanes] = pairs[t][1].astype(BF)
                    mixed = [mix(halves[two][split + duo * SUB:split + (duo + 1) * SUB]) for two in range(2)]
                    for t in range(3):
                        spread[tail_at + four * TALL:tail_at + (four + 1) * TALL, (3 * duo + t) * LANES:(3 * duo + t + 1) * LANES] = (
                            jnp.concatenate([mixed[0][t], mixed[1][t]], axis=0).astype(BF)
                        )

        def contract_right(block):
            done = jnp.dot(spread[...], right_rows[slot], preferred_element_type=F32) * scaling[...]
            total[...] += jnp.sum((done * done).reshape(-1, SUB, 2 * LANES), axis=0)
            for s in range(2):
                out[s] = done[:, s * LANES:(s + 1) * LANES]
            at = pl.multiple_of(block * 2 * SUB, 2 * SUB)
            for quad in range(pair // 4):
                lines = []
                for leg in range(4 * quad, 4 * quad + 4):
                    if leg < TALL:
                        place = pl.ds(leg, SUB, stride=TALL)
                    else:
                        place = pl.ds(tail_at + leg - TALL, SUB, stride=high_legs)
                    lines.append([out[s, place, :] for s in range(2)])
                both = []
                for s in range(2):
                    moved = [
                        lane_roll(lines[leg][s], (-leg) % 4 * UNIT) for leg in range(4)
                    ]
                    both.append([
                        jnp.where(lane_unit < 3 - t, moved[t], moved[t + 1]) for t in range(3)
                    ])
                for t in range(3):
                    lanes = slice((3 * quad + t) * LANES, (3 * quad + t + 1) * LANES)
                    for s in range(2):
                        grown[pl.ds(pl.multiple_of(s * half + block * SUB, SUB), SUB), lanes] = both[s][t]
                    landed[FAR, pl.ds(at, 2 * SUB), lanes] = jnp.concatenate([both[0][t], both[1][t]], axis=0).astype(BF)

        contract_left(first_group * GROUP)

        def one_group(group, carry):
            for step in range(GROUP):
                block = group * GROUP + step
                contract_site()
                if step == 0:
                    @pl.when(sends & (group > first_group))
                    def _():
                        copy_of(which, block - 1, place).start()
                if step == GROUP - 1:
                    @pl.when(sends)
                    def _():
                        for done in range(step):
                            copy_of(which, block - step + done, place).start()
                if step < GROUP - 1:
                    contract_left(block + 1)
                else:
                    @pl.when(group < last_group - 1)
                    def _():
                        contract_left(block + 1)
                contract_right(block)
            return carry

        lax.fori_loop(first_group, last_group, one_group, 0)

        @pl.when(sends)
        def _():
            copy_of(which, last_group * GROUP - 1, place).start()

    def collect(which):
        squares = total[:, :LANES] + total[:, LANES:]
        for block in range(blocks // 2, blocks):
            copy_of(which, block).wait_recv()
        for block in range(blocks // 2, blocks):
            for lanes in range(0, pair * chi, LANES):
                values = landed[which, block * 2 * SUB:(block + 1) * 2 * SUB, lanes:lanes + LANES].astype(F32)
                for s in range(2):
                    value = values[s * SUB:(s + 1) * SUB]
                    squares += value * value
                    grown[s * half + block * SUB:s * half + (block + 1) * SUB, lanes:lanes + LANES] = value
        total[:, :LANES] = squares
        total[:, LANES:] = jnp.zeros((SUB, LANES), F32)

    def one_turn(turn, carry):
        last = turn == rows - 1
        owns = (row == turn) | (row == rows - 1 - turn)
        helps = last & helping if split else jnp.bool_(False)
        finishes = last & owns if split else jnp.bool_(False)
        sends = jnp.logical_not(last & owns)
        active = owns | helps
        which = jnp.where(row == jnp.where(helps, rows - 2, turn), 0, 1)
        slot = jnp.where(helps, FAR, which)
        place = jnp.where(helps, 1 - which, which)
        first_group = jnp.where(helps, 1, 0)
        last_group = jnp.where(finishes, 1, groups)
        early = jnp.where((row == 0) | (row == rows - 1), 1, 2)

        def one_prepare(step, carry):
            mine = jnp.where(step == 0, begin, 1 - begin)
            prepare(mine)
            prepare_left(mine)
            if split:
                @pl.when(outer & (step == 1))
                def _():
                    far_copy(1).start()
                    far_copy(2).start()

            return carry

        @pl.when(turn == 0)
        def _():
            copy_in(tensor_hbm, tensor, 0).wait()
            copy_in(right_hbm, right, 1).wait()
            copy_in(top_hbm, held, 2).wait()

        @pl.when(active & (turn == 0))
        def _():
            for lanes in range(0, pair * chi, LANES):
                landed[which, :, lanes:lanes + LANES] = permuted(held[:, lanes:lanes + LANES].astype(F32)).astype(BF)

        lax.fori_loop(
            jnp.where(turn == 0, 0, jnp.where(turn == 1, early, 2)), jnp.where(turn == 0, early, 2), one_prepare, 0
        )

        if split:
            @pl.when(helping & (turn == 0))
            def _():
                far_copy(0).wait_recv()
                lay_right(FAR, lambda lanes: right_far[:, lanes])

        @pl.when(helps)
        def _():
            far_copy(1).wait_recv()
            far_copy(2).wait_recv()

        @pl.when(active)
        def _():
            def one_unpack(block, squares):
                @pl.when((turn > 0) & jnp.logical_not(helps))
                def _():
                    copy_of(which, block).wait_recv()

                return squares + unpack(slot, block)

            squares = lax.fori_loop(0, blocks, one_unpack, jnp.zeros((SUB, LANES), F32))
            norm = jnp.where(turn > 0, inverse_norm(squares), jnp.ones((1, 1), F32))
            scaling[...] = jnp.broadcast_to(norm, scaling.shape)
            absorb(which, slot, place, sends, first_group, last_group)

        @pl.when(finishes)
        def _():
            collect(1 - which)

        @pl.when(owns)
        def _():
            env_ref[which] = (grown[...] * inverse_norm(total[...])).astype(BF)

        @pl.when(active & sends)
        def _():
            def one_wait(block, carry):
                copy_of(which, block, place).wait_send()
                return carry

            lax.fori_loop(first_group * GROUP, blocks, one_wait, 0)

        return carry

    lax.fori_loop(0, rows, one_turn, 0)
    if split:
        @pl.when(outer)
        def _():
            for item in range(3):
                far_copy(item).wait_send()

    for which in range(2):
        for chunk in range(chunks):
            left_copy(which, chunk).wait_send()


def sweep(rows, cols, top, bottom, tensor, left, right, chi, pair):
    slab = round_up(pair * round_up(pair, SUB), LANES)
    count = pair * pair
    half = chi // 2
    blocks = half // SUB
    lanes = pair // 2 * 3 * LANES
    return pl.pallas_call(
        functools.partial(sweep_kernel, rows, cols, chi, pair),
        out_shape=jax.ShapeDtypeStruct((2,) + top.shape, top.dtype),
        in_specs=[pl.BlockSpec(memory_space=pltpu.HBM)] * 5,
        out_specs=pl.BlockSpec(memory_space=pltpu.VMEM),
        scratch_shapes=[
            pltpu.VMEM(tensor.shape, BF),
            pltpu.VMEM(right.shape, BF),
            pltpu.VMEM(top.shape, BF),
            pltpu.VMEM(left.shape, BF),
            pltpu.VMEM((slab // LANES, slab, LANES), F32),
            pltpu.VMEM((slab // LANES, slab, LANES), F32),
            pltpu.VMEM((slab, slab), F32),
            pltpu.VMEM((3, count, count), BF),
            pltpu.VMEM((2, half * pair, LANES), F32),
            pltpu.VMEM((3, half * pair, 2 * LANES), BF),
            pltpu.VMEM((3, lanes, 2 * LANES), BF),
            pltpu.VMEM((2 * LANES, lanes), BF),
            pltpu.VMEM((count, SUB // 2 * 3 * LANES), BF),
            pltpu.VMEM((SUB * pair, lanes), BF),
            pltpu.VMEM((2, SUB * pair, LANES), F32),
            pltpu.VMEM(top.shape, F32),
            pltpu.VMEM((SUB, 2 * LANES), F32),
            pltpu.VMEM((3,) + top.shape, BF),
            pltpu.VMEM((1, 2 * LANES), F32),
            pltpu.VMEM(top.shape, BF),
            pltpu.SemaphoreType.DMA((3,)),
            pltpu.SemaphoreType.DMA((2, pair // 4)),
            pltpu.SemaphoreType.DMA((2, pair // 4)),
            pltpu.SemaphoreType.DMA((blocks,)),
            pltpu.SemaphoreType.DMA((2, blocks)),
            pltpu.SemaphoreType.DMA((3,)),
            pltpu.SemaphoreType.DMA((3,)),
        ],
        compiler_params=pltpu.CompilerParams(collective_id=0, has_side_effects=True, vmem_limit_bytes=40 * 1024 * 1024),
        name="sweep",
    )(*[pltpu.with_memory_space_constraint(x, pltpu.HBM) for x in (top, bottom, tensor, left, right)])


def local(top_in, bottom_in, row_tensor, left_proj, right_proj):
    chi = top_in.shape[1]
    pair = row_tensor.shape[2]
    env = sweep(
        lax.axis_size("row"), lax.axis_size("col"), top_in[0], bottom_in[0], row_tensor[0, 0],
        left_proj[:, 0, 0], right_proj[:, 0, 0], chi, pair,
    )
    return env[:, None, None]


def solution(mesh):
    return jax.shard_map(
        local,
        mesh=mesh,
        in_specs=(
            P("col", None, None),
            P("col", None, None),
            P("row", "col", None, None, None),
            P(None, "row", "col", None, None),
            P(None, "row", "col", None, None),
        ),
        out_specs=P(None, "row", "col", None, None),
        check_vma=False,
    )
```

```python
import functools

import jax
import jax.numpy as jnp
from jax import lax
from jax.experimental import pallas as pl
from jax.experimental.pallas import tpu as pltpu
from jax.sharding import PartitionSpec as P

epsilon = 1e-06
LANES = 128
WIDE = 64
UNIT = 32
SUB = 8
TALL = 16
GROUP = 3
FAR = 2
BF = jnp.bfloat16
F32 = jnp.float32


def round_up(value, unit):
    return -(-value // unit) * unit


def lane_roll(value, amount):
    return pltpu.roll(value, amount, 1) if amount else value


def sweep_kernel(rows, cols, chi, pair, top_hbm, bottom_hbm, tensor_hbm, left_hbm, right_hbm, env_ref,
                 tensor, right, held, leftraw, tall, turned, pieces, site, left_tall, left_rows, right_rows,
                 wide, first, spread, out, grown, total, landed, scaling, right_far,
                 local_sem, left_send, left_recv, send_sem, recv_sem, far_send, far_recv):
    row = lax.axis_index("row")
    col = lax.axis_index("col")
    half = chi // 2
    blocks = half // SUB
    groups = blocks // GROUP
    low_legs = TALL
    high_legs = pair - TALL
    block_rows = SUB * pair
    tail_at = SUB * TALL
    padded = round_up(pair, SUB)
    bond = chi * 4
    chunks = pair // 4
    begin = jnp.where(row < rows // 2, 0, 1)
    split = rows > 2

    def copy_in(source, target, at):
        return pltpu.make_async_copy(source, target, local_sem.at[at])

    copy_in(tensor_hbm, tensor, 0).start()
    copy_in(right_hbm, right, 1).start()

    @pl.when(row < rows // 2)
    def _():
        copy_in(top_hbm, held, 2).start()

    @pl.when(row >= rows // 2)
    def _():
        copy_in(bottom_hbm, held, 2).start()

    barrier = pltpu.get_barrier_semaphore()
    for step in (1, cols - 1):
        pl.semaphore_signal(barrier, inc=1, device_id={"col": lax.rem(col + step, cols)}, device_id_type=pl.DeviceIdType.MESH)

    @pl.when(row > 0)
    def _():
        pl.semaphore_signal(barrier, inc=1, device_id={"row": row - 1}, device_id_type=pl.DeviceIdType.MESH)

    @pl.when(row < rows - 1)
    def _():
        pl.semaphore_signal(barrier, inc=1, device_id={"row": row + 1}, device_id_type=pl.DeviceIdType.MESH)

    pl.semaphore_wait(barrier, 2 + jnp.where(row > 0, 1, 0) + jnp.where(row < rows - 1, 1, 0))

    def left_copy(which, chunk):
        return pltpu.make_async_remote_copy(
            src_ref=left_hbm.at[which, :, pl.ds(chunk * bond, bond)],
            dst_ref=leftraw.at[which, :, pl.ds(chunk * bond, bond)],
            send_sem=left_send.at[which, chunk],
            recv_sem=left_recv.at[which, chunk],
            device_id={"col": lax.rem(col + 1, cols)},
            device_id_type=pl.DeviceIdType.MESH,
        )

    outer = (row == 0) | (row == rows - 1)
    helping = (row == 1) | (row == rows - 2)
    inward = jnp.where(row < rows // 2, row + 1, row - 1)
    cut = blocks // 2 * block_rows

    def far_copy(item):
        mine = 1 - begin
        source, target = (
            (right_hbm.at[mine], right_far),
            (site.at[mine], site.at[FAR]),
            (left_rows.at[mine, pl.ds(cut, cut)], left_rows.at[FAR, pl.ds(cut, cut)]),
        )[item]
        return pltpu.make_async_remote_copy(
            src_ref=source,
            dst_ref=target,
            send_sem=far_send.at[item],
            recv_sem=far_recv.at[item],
            device_id={"row": inward},
            device_id_type=pl.DeviceIdType.MESH,
        )

    for chunk in range(chunks):
        left_copy(begin, chunk).start()

    if split:
        @pl.when(outer)
        def _():
            far_copy(0).start()

    for chunk in range(chunks):
        left_copy(1 - begin, chunk).start()

    wide[...] = jnp.zeros_like(wide)
    right_rows[...] = jnp.zeros_like(right_rows)
    left_tall[...] = jnp.zeros_like(left_tall)
    tall[...] = jnp.zeros_like(tall)
    pieces[...] = jnp.zeros_like(pieces)

    lane_unit = lax.broadcasted_iota(jnp.int32, (SUB, LANES), 1) // UNIT
    low = lane_unit < 2
    low_tall = (lax.broadcasted_iota(jnp.int32, (TALL, LANES), 1) // UNIT) < 2
    sub = lax.broadcasted_iota(jnp.int32, (SUB, LANES), 0) < SUB // 2
    diag = low == sub
    tall_unit = lax.broadcasted_iota(jnp.int32, (TALL, LANES), 1) // UNIT

    def swap_lanes(value):
        return pltpu.roll(value, WIDE, 1)

    def swap_sub(value):
        return pltpu.roll(value, SUB // 2, 0)

    def order(index):
        split = pair * TALL
        later = index - split
        big = jnp.where(index < split, index // TALL, later // high_legs)
        small = jnp.where(index < split, index % TALL, TALL + later % high_legs)
        return big, small

    def permuted(value):
        return jnp.concatenate(
            [value[s * half + k * SUB:s * half + (k + 1) * SUB] for k in range(blocks) for s in range(2)], axis=0
        )

    def lay_right(slot, load):
        for leg in range(pair):
            base = (leg // 2) * 3 * LANES
            block = load(slice(leg * chi, (leg + 1) * chi))
            for s in range(2):
                at = base + (leg % 2) * LANES + s * WIDE
                right_rows[slot, at:at + WIDE, s * LANES:s * LANES + chi] = block[:WIDE]
                at = base + 2 * LANES + (leg % 2) * WIDE + s * UNIT
                right_rows[slot, at:at + UNIT, s * LANES:s * LANES + chi] = block[WIDE:]

    def prepare(which):
        slabs, slab, _ = tall.shape
        count = pair * pair
        for leg in range(pair):
            plane = tensor[leg].astype(F32)
            for part in range(slabs):
                lanes = min(LANES, count - part * LANES)
                tall[part, pl.ds(leg, pair, stride=padded), :lanes] = plane[:, part * LANES:part * LANES + lanes]
        for part in range(slabs):
            for other in range(slabs):
                turned[other, part * LANES:(part + 1) * LANES, :] = tall[part, other * LANES:(other + 1) * LANES, :].T
        big, small = order(lax.broadcasted_iota(jnp.int32, (1, count), 1))
        pick_lanes = (lax.broadcasted_iota(jnp.int32, (slab, count), 0) == big * padded + small).astype(F32).astype(BF)
        big, small = order(lax.broadcasted_iota(jnp.int32, (count, 1), 0))

        def finish(source, wanted):
            pick_rows = (lax.broadcasted_iota(jnp.int32, (count, slab), 1) == wanted).astype(F32).astype(BF)
            ordered = jnp.dot(pick_rows, source.astype(BF), preferred_element_type=F32).astype(BF)
            site[which] = jnp.dot(ordered, pick_lanes, preferred_element_type=F32).astype(BF)

        @pl.when(which == 0)
        def _():
            finish(jnp.concatenate([turned[part] for part in range(slabs)], axis=1), big * pair + small)

        @pl.when(which == 1)
        def _():
            for near in range(pair):
                lines = jnp.concatenate([turned[part, pl.ds(near, pair, stride=pair), :] for part in range(slabs)], axis=1)
                for far in range(pair):
                    pieces[far * padded:far * padded + pair, near * padded:(near + 1) * padded] = (
                        lines[:, far * padded:(far + 1) * padded]
                    )
            finish(pieces[...], small * padded + big)

        lay_right(which, lambda lanes: right[which, :, lanes])

    def prepare_left(which):
        for leg in range(pair):
            if leg % 4 == 0:
                left_copy(which, leg // 4).wait_recv()
            block = permuted(leftraw[which, :, leg * chi:(leg + 1) * chi].astype(F32)).T
            for k in range(blocks):
                for s in range(2):
                    piece = block[s * half + k * SUB:s * half + (k + 1) * SUB]
                    if leg < TALL:
                        place = pl.ds(k * block_rows + leg, SUB, stride=TALL)
                    else:
                        place = pl.ds(k * block_rows + tail_at + leg - TALL, SUB, stride=high_legs)
                    left_tall[s, place, :chi] = piece
        for s in range(2):
            left_rows[which, :, s * LANES:(s + 1) * LANES] = left_tall[s].astype(BF)

    def copy_of(which, block, place=None):
        at = pl.multiple_of(block * 2 * SUB, 2 * SUB)
        return pltpu.make_async_remote_copy(
            src_ref=landed.at[FAR, pl.ds(at, 2 * SUB)],
            dst_ref=landed.at[which if place is None else place, pl.ds(at, 2 * SUB)],
            send_sem=send_sem.at[block],
            recv_sem=recv_sem.at[which if place is None else place, block],
            device_id={"row": jnp.where(which == 0, row + 1, row - 1)},
            device_id_type=pl.DeviceIdType.MESH,
        )

    def inverse_norm(square_sum):
        return lax.rsqrt(jnp.full((1, 1), jnp.sum(square_sum) / (chi * pair * chi) + epsilon, F32))

    def unpack(source_at, block):
        at = pl.multiple_of(block * 2 * SUB, 2 * SUB)
        squares = jnp.zeros((SUB, LANES), F32)
        for quad in range(pair // 4):
            tiles = [
                landed[source_at, pl.ds(at, 2 * SUB), (3 * quad + t) * LANES:(3 * quad + t + 1) * LANES]
                for t in range(3)
            ]
            for tile in tiles:
                value = tile.astype(F32)
                squares += jnp.sum((value * value).reshape(2, SUB, LANES), axis=0)

            def unit(leg, part, place):
                source, position = divmod(leg * 3 + part, 4)
                return lane_roll(tiles[source], (place - position) % 4 * UNIT)

            def build(parts, s):
                value = jnp.zeros((TALL, LANES), BF)
                for leg, part, place in parts:
                    value = jnp.where(tall_unit == place, unit(leg, part, place), value)
                return value

            for s in range(2):
                for duo in range(2):
                    base = (2 * quad + duo) * 3 * LANES
                    for v in range(2):
                        leg = 2 * duo + v
                        wide[pl.ds(pl.multiple_of(s * LANES + at, TALL), TALL), base + v * LANES:base + (v + 1) * LANES] = (
                            build([(leg, 0, 2 * s), (leg, 1, 2 * s + 1)], s)
                        )
                    wide[pl.ds(pl.multiple_of(s * LANES + at, TALL), TALL), base + 2 * LANES:base + 3 * LANES] = (
                        build([(2 * duo, 2, s), (2 * duo + 1, 2, 2 + s)], s)
                    )
        return squares

    def mix(tile):
        p, q, x = tile[:, :LANES], tile[:, LANES:2 * LANES], tile[:, 2 * LANES:]
        return (
            jnp.where(sub, p, swap_sub(q)),
            jnp.where(sub, swap_sub(p), q),
            jnp.where(diag, x, swap_lanes(swap_sub(x))),
        )

    def cross(upper, lower):
        x, y = upper[:, 2 * LANES:], lower[:, 2 * LANES:]
        return jnp.where(low_tall, x, swap_lanes(y)), jnp.where(low_tall, swap_lanes(x), y)

    def absorb(which, slot, place, sends, first_group, last_group):
        total[...] = jnp.zeros_like(total)
        split = pair * TALL

        def contract_left(block):
            left_here = left_rows[slot, pl.ds(pl.multiple_of(block * block_rows, block_rows), block_rows), :]
            for quad in range(pair // 4):
                part = jnp.dot(left_here, wide[:, quad * 6 * LANES:(quad + 1) * 6 * LANES], preferred_element_type=F32)
                halves = [part[:, :3 * LANES], part[:, 3 * LANES:]]
                for duo in range(2):
                    at = (2 * quad + duo) * 2 * TALL
                    for two in range(SUB // 2):
                        upper = halves[duo][2 * two * TALL:(2 * two + 1) * TALL]
                        lower = halves[duo][(2 * two + 1) * TALL:(2 * two + 2) * TALL]
                        pairs = (
                            (upper[:, :LANES], upper[:, LANES:2 * LANES]),
                            (lower[:, :LANES], lower[:, LANES:2 * LANES]),
                            cross(upper, lower),
                        )
                        for t in range(3):
                            lanes = slice((3 * two + t) * LANES, (3 * two + t + 1) * LANES)
                            first[at:at + TALL, lanes] = pairs[t][0].astype(BF)
                            first[at + TALL:at + 2 * TALL, lanes] = pairs[t][1].astype(BF)
                for two in range(SUB // 2):
                    mixed = [mix(halves[duo][tail_at + two * SUB:tail_at + (two + 1) * SUB]) for duo in range(2)]
                    for t in range(3):
                        first[split + quad * TALL:split + (quad + 1) * TALL, (3 * two + t) * LANES:(3 * two + t + 1) * LANES] = (
                            jnp.concatenate([mixed[0][t], mixed[1][t]], axis=0).astype(BF)
                        )

        def contract_site():
            for four in range(SUB // 4):
                part = jnp.dot(site[slot], first[:, four * 6 * LANES:(four + 1) * 6 * LANES], preferred_element_type=F32)
                halves = [part[:, :3 * LANES], part[:, 3 * LANES:]]
                for duo in range(pair // 2):
                    for two in range(2):
                        at = (4 * four + 2 * two) * TALL
                        upper = halves[two][2 * duo * TALL:(2 * duo + 1) * TALL]
                        lower = halves[two][(2 * duo + 1) * TALL:(2 * duo + 2) * TALL]
                        pairs = (
                            (upper[:, :LANES], upper[:, LANES:2 * LANES]),
                            (lower[:, :LANES], lower[:, LANES:2 * LANES]),
                            cross(upper, lower),
                        )
                        for t in range(3):
                            lanes = slice((3 * duo + t) * LANES, (3 * duo + t + 1) * LANES)
                            spread[at:at + TALL, lanes] = pairs[t][0].astype(BF)
                            spread[at + TALL:at + 2 * TALL, lanes] = pairs[t][1].astype(BF)
                    mixed = [mix(halves[two][split + duo * SUB:split + (duo + 1) * SUB]) for two in range(2)]
                    for t in range(3):
                        spread[tail_at + four * TALL:tail_at + (four + 1) * TALL, (3 * duo + t) * LANES:(3 * duo + t + 1) * LANES] = (
                            jnp.concatenate([mixed[0][t], mixed[1][t]], axis=0).astype(BF)
                        )

        def contract_right(block):
            done = jnp.dot(spread[...], right_rows[slot], preferred_element_type=F32) * scaling[...]
            total[...] += jnp.sum((done * done).reshape(-1, SUB, 2 * LANES), axis=0)
            for s in range(2):
                out[s] = done[:, s * LANES:(s + 1) * LANES]
            at = pl.multiple_of(block * 2 * SUB, 2 * SUB)
            for quad in range(pair // 4):
                lines = []
                for leg in range(4 * quad, 4 * quad + 4):
                    if leg < TALL:
                        place = pl.ds(leg, SUB, stride=TALL)
                    else:
                        place = pl.ds(tail_at + leg - TALL, SUB, stride=high_legs)
                    lines.append([out[s, place, :] for s in range(2)])
                both = []
                for s in range(2):
                    moved = [
                        lane_roll(lines[leg][s], (-leg) % 4 * UNIT) for leg in range(4)
                    ]
                    both.append([
                        jnp.where(lane_unit < 3 - t, moved[t], moved[t + 1]) for t in range(3)
                    ])
                for t in range(3):
                    lanes = slice((3 * quad + t) * LANES, (3 * quad + t + 1) * LANES)
                    for s in range(2):
                        grown[pl.ds(pl.multiple_of(s * half + block * SUB, SUB), SUB), lanes] = both[s][t]
                    landed[FAR, pl.ds(at, 2 * SUB), lanes] = jnp.concatenate([both[0][t], both[1][t]], axis=0).astype(BF)

        def one_group(group, carry):
            for step in range(GROUP):
                block = group * GROUP + step
                if step == 0:
                    contract_left(block)
                contract_site()
                if step < GROUP - 1:
                    contract_left(block + 1)
                else:
                    @pl.when(sends)
                    def _():
                        for done in range(step):
                            copy_of(which, block - step + done, place).start()
                contract_right(block)

            @pl.when(sends)
            def _():
                copy_of(which, group * GROUP + GROUP - 1, place).start()

            return carry

        lax.fori_loop(first_group, last_group, one_group, 0)

    def collect(which):
        squares = total[:, :LANES] + total[:, LANES:]
        for block in range(blocks // 2, blocks):
            copy_of(which, block).wait_recv()
        for block in range(blocks // 2, blocks):
            for lanes in range(0, pair * chi, LANES):
                values = landed[which, block * 2 * SUB:(block + 1) * 2 * SUB, lanes:lanes + LANES].astype(F32)
                for s in range(2):
                    value = values[s * SUB:(s + 1) * SUB]
                    squares += value * value
                    grown[s * half + block * SUB:s * half + (block + 1) * SUB, lanes:lanes + LANES] = value
        total[:, :LANES] = squares
        total[:, LANES:] = jnp.zeros((SUB, LANES), F32)

    def one_turn(turn, carry):
        last = turn == rows - 1
        owns = (row == turn) | (row == rows - 1 - turn)
        helps = last & helping if split else jnp.bool_(False)
        finishes = last & owns if split else jnp.bool_(False)
        sends = jnp.logical_not(last & owns)
        active = owns | helps
        which = jnp.where(row == jnp.where(helps, rows - 2, turn), 0, 1)
        slot = jnp.where(helps, FAR, which)
        place = jnp.where(helps, 1 - which, which)
        first_group = jnp.where(helps, 1, 0)
        last_group = jnp.where(finishes, 1, groups)
        early = jnp.where((row == 0) | (row == rows - 1), 1, 2)

        def one_prepare(step, carry):
            mine = jnp.where(step == 0, begin, 1 - begin)
            prepare(mine)
            return carry

        def one_prepare_left(step, carry):
            mine = jnp.where(step == 0, begin, 1 - begin)
            prepare_left(mine)
            if split:
                @pl.when(outer & (step == 1))
                def _():
                    far_copy(1).start()
                    far_copy(2).start()

            return carry

        @pl.when(turn == 0)
        def _():
            copy_in(tensor_hbm, tensor, 0).wait()
            copy_in(right_hbm, right, 1).wait()
            copy_in(top_hbm, held, 2).wait()

        @pl.when(active & (turn == 0))
        def _():
            for lanes in range(0, pair * chi, LANES):
                landed[which, :, lanes:lanes + LANES] = permuted(held[:, lanes:lanes + LANES].astype(F32)).astype(BF)

        from_step = jnp.where(turn == 0, 0, jnp.where(turn == 1, early, 2))
        to_step = jnp.where(turn == 0, early, 2)
        lax.fori_loop(from_step, to_step, one_prepare, 0)

        @pl.when(active)
        def _():
            def one_unpack(block, squares):
                @pl.when((turn > 0) & jnp.logical_not(helps))
                def _():
                    copy_of(which, block).wait_recv()

                return squares + unpack(slot, block)

            squares = lax.fori_loop(0, blocks, one_unpack, jnp.zeros((SUB, LANES), F32))
            norm = jnp.where(turn > 0, inverse_norm(squares), jnp.ones((1, 1), F32))
            scaling[...] = jnp.broadcast_to(norm, scaling.shape)

        lax.fori_loop(from_step, to_step, one_prepare_left, 0)

        if split:
            @pl.when(helping & (turn == 0))
            def _():
                far_copy(0).wait_recv()
                lay_right(FAR, lambda lanes: right_far[:, lanes])

        @pl.when(helps)
        def _():
            far_copy(1).wait_recv()
            far_copy(2).wait_recv()

        @pl.when(active & (turn > jnp.minimum(row, rows - 1 - row)))
        def _():
            for block in range(blocks):
                copy_of(which, block).wait_send()

        @pl.when(active)
        def _():
            absorb(which, slot, place, sends, first_group, last_group)

        @pl.when(finishes)
        def _():
            collect(1 - which)

        @pl.when(owns)
        def _():
            env_ref[which] = (grown[...] * inverse_norm(total[...])).astype(BF)

        return carry

    lax.fori_loop(0, rows, one_turn, 0)

    def one_wait(block, carry):
        copy_of(begin, block).wait_send()
        return carry

    lax.fori_loop(jnp.where(outer, blocks, jnp.where(helping, blocks // 2, 0)), blocks, one_wait, 0)
    if split:
        @pl.when(outer)
        def _():
            for item in range(3):
                far_copy(item).wait_send()

    for which in range(2):
        for chunk in range(chunks):
            left_copy(which, chunk).wait_send()


def sweep(rows, cols, top, bottom, tensor, left, right, chi, pair):
    slab = round_up(pair * round_up(pair, SUB), LANES)
    count = pair * pair
    half = chi // 2
    blocks = half // SUB
    lanes = pair // 2 * 3 * LANES
    return pl.pallas_call(
        functools.partial(sweep_kernel, rows, cols, chi, pair),
        out_shape=jax.ShapeDtypeStruct((2,) + top.shape, top.dtype),
        in_specs=[pl.BlockSpec(memory_space=pltpu.HBM)] * 5,
        out_specs=pl.BlockSpec(memory_space=pltpu.VMEM),
        scratch_shapes=[
            pltpu.VMEM(tensor.shape, BF),
            pltpu.VMEM(right.shape, BF),
            pltpu.VMEM(top.shape, BF),
            pltpu.VMEM(left.shape, BF),
            pltpu.VMEM((slab // LANES, slab, LANES), F32),
            pltpu.VMEM((slab // LANES, slab, LANES), F32),
            pltpu.VMEM((slab, slab), F32),
            pltpu.VMEM((3, count, count), BF),
            pltpu.VMEM((2, half * pair, LANES), F32),
            pltpu.VMEM((3, half * pair, 2 * LANES), BF),
            pltpu.VMEM((3, lanes, 2 * LANES), BF),
            pltpu.VMEM((2 * LANES, lanes), BF),
            pltpu.VMEM((count, SUB // 2 * 3 * LANES), BF),
            pltpu.VMEM((SUB * pair, lanes), BF),
            pltpu.VMEM((2, SUB * pair, LANES), F32),
            pltpu.VMEM(top.shape, F32),
            pltpu.VMEM((SUB, 2 * LANES), F32),
            pltpu.VMEM((3,) + top.shape, BF),
            pltpu.VMEM((1, 2 * LANES), F32),
            pltpu.VMEM(top.shape, BF),
            pltpu.SemaphoreType.DMA((3,)),
            pltpu.SemaphoreType.DMA((2, pair // 4)),
            pltpu.SemaphoreType.DMA((2, pair // 4)),
            pltpu.SemaphoreType.DMA((blocks,)),
            pltpu.SemaphoreType.DMA((2, blocks)),
            pltpu.SemaphoreType.DMA((3,)),
            pltpu.SemaphoreType.DMA((3,)),
        ],
        compiler_params=pltpu.CompilerParams(collective_id=0, has_side_effects=True, vmem_limit_bytes=40 * 1024 * 1024),
        name="sweep",
    )(*[pltpu.with_memory_space_constraint(x, pltpu.HBM) for x in (top, bottom, tensor, left, right)])


def local(top_in, bottom_in, row_tensor, left_proj, right_proj):
    chi = top_in.shape[1]
    pair = row_tensor.shape[2]
    env = sweep(
        lax.axis_size("row"), lax.axis_size("col"), top_in[0], bottom_in[0], row_tensor[0, 0],
        left_proj[:, 0, 0], right_proj[:, 0, 0], chi, pair,
    )
    return env[:, None, None]


def solution(mesh):
    return jax.shard_map(
        local,
        mesh=mesh,
        in_specs=(
            P("col", None, None),
            P("col", None, None),
            P("row", "col", None, None, None),
            P(None, "row", "col", None, None),
            P(None, "row", "col", None, None),
        ),
        out_specs=P(None, "row", "col", None, None),
        check_vma=False,
    )
```

```python
import functools

import jax
import jax.numpy as jnp
from jax import lax
from jax.experimental import pallas as pl
from jax.experimental.pallas import tpu as pltpu
from jax.sharding import PartitionSpec as P

epsilon = 1e-06
LANES = 128
WIDE = 64
UNIT = 32
SUB = 8
TALL = 16
GROUP = 3
FAR = 2
BF = jnp.bfloat16
F32 = jnp.float32


def round_up(value, unit):
    return -(-value // unit) * unit


def lane_roll(value, amount):
    return pltpu.roll(value, amount, 1) if amount else value


def sweep_kernel(rows, cols, chi, pair, top_hbm, bottom_hbm, tensor_hbm, left_hbm, right_hbm, env_ref,
                 tensor, right, held, leftraw, tall, turned, pieces, site, left_tall, left_rows, right_rows,
                 wide, first, spread, out, grown, total, landed, scaling, right_far,
                 local_sem, left_send, left_recv, send_sem, recv_sem, far_send, far_recv):
    row = lax.axis_index("row")
    col = lax.axis_index("col")
    half = chi // 2
    blocks = half // SUB
    groups = blocks // GROUP
    low_legs = TALL
    high_legs = pair - TALL
    block_rows = SUB * pair
    tail_at = SUB * TALL
    padded = round_up(pair, SUB)
    bond = chi * 4
    chunks = pair // 4
    begin = jnp.where(row < rows // 2, 0, 1)
    split = rows > 2

    def copy_in(source, target, at):
        return pltpu.make_async_copy(source, target, local_sem.at[at])

    copy_in(tensor_hbm, tensor, 0).start()
    copy_in(right_hbm, right, 1).start()

    @pl.when(row < rows // 2)
    def _():
        copy_in(top_hbm, held, 2).start()

    @pl.when(row >= rows // 2)
    def _():
        copy_in(bottom_hbm, held, 2).start()

    barrier = pltpu.get_barrier_semaphore()
    for step in (1, cols - 1):
        pl.semaphore_signal(barrier, inc=1, device_id={"col": lax.rem(col + step, cols)}, device_id_type=pl.DeviceIdType.MESH)

    @pl.when(row > 0)
    def _():
        pl.semaphore_signal(barrier, inc=1, device_id={"row": row - 1}, device_id_type=pl.DeviceIdType.MESH)

    @pl.when(row < rows - 1)
    def _():
        pl.semaphore_signal(barrier, inc=1, device_id={"row": row + 1}, device_id_type=pl.DeviceIdType.MESH)

    wide[...] = jnp.zeros_like(wide)
    right_rows[...] = jnp.zeros_like(right_rows)
    left_tall[...] = jnp.zeros_like(left_tall)
    tall[...] = jnp.zeros_like(tall)
    pieces[...] = jnp.zeros_like(pieces)

    pl.semaphore_wait(barrier, 2 + jnp.where(row > 0, 1, 0) + jnp.where(row < rows - 1, 1, 0))

    def left_copy(which, chunk):
        return pltpu.make_async_remote_copy(
            src_ref=left_hbm.at[which, :, pl.ds(chunk * bond, bond)],
            dst_ref=leftraw.at[which, :, pl.ds(chunk * bond, bond)],
            send_sem=left_send.at[which, chunk],
            recv_sem=left_recv.at[which, chunk],
            device_id={"col": lax.rem(col + 1, cols)},
            device_id_type=pl.DeviceIdType.MESH,
        )

    outer = (row == 0) | (row == rows - 1)
    helping = (row == 1) | (row == rows - 2)
    inward = jnp.where(row < rows // 2, row + 1, row - 1)
    cut = blocks // 2 * block_rows

    def far_copy(item):
        mine = 1 - begin
        source, target = (
            (right_hbm.at[mine], right_far),
            (site.at[mine], site.at[FAR]),
            (left_rows.at[mine, pl.ds(cut, cut)], left_rows.at[FAR, pl.ds(cut, cut)]),
        )[item]
        return pltpu.make_async_remote_copy(
            src_ref=source,
            dst_ref=target,
            send_sem=far_send.at[item],
            recv_sem=far_recv.at[item],
            device_id={"row": inward},
            device_id_type=pl.DeviceIdType.MESH,
        )

    for chunk in range(chunks):
        left_copy(begin, chunk).start()

    if split:
        @pl.when(outer)
        def _():
            far_copy(0).start()

    for chunk in range(chunks):
        left_copy(1 - begin, chunk).start()


    lane_unit = lax.broadcasted_iota(jnp.int32, (SUB, LANES), 1) // UNIT
    low = lane_unit < 2
    low_tall = (lax.broadcasted_iota(jnp.int32, (TALL, LANES), 1) // UNIT) < 2
    sub = lax.broadcasted_iota(jnp.int32, (SUB, LANES), 0) < SUB // 2
    diag = low == sub
    tall_unit = lax.broadcasted_iota(jnp.int32, (TALL, LANES), 1) // UNIT

    def swap_lanes(value):
        return pltpu.roll(value, WIDE, 1)

    def swap_sub(value):
        return pltpu.roll(value, SUB // 2, 0)

    def order(index):
        split = pair * TALL
        later = index - split
        big = jnp.where(index < split, index // TALL, later // high_legs)
        small = jnp.where(index < split, index % TALL, TALL + later % high_legs)
        return big, small

    def permuted(value):
        return jnp.concatenate(
            [value[s * half + k * SUB:s * half + (k + 1) * SUB] for k in range(blocks) for s in range(2)], axis=0
        )

    def lay_right(slot, load):
        for leg in range(pair):
            base = (leg // 2) * 3 * LANES
            block = load(slice(leg * chi, (leg + 1) * chi))
            for s in range(2):
                at = base + (leg % 2) * LANES + s * WIDE
                right_rows[slot, at:at + WIDE, s * LANES:s * LANES + chi] = block[:WIDE]
                at = base + 2 * LANES + (leg % 2) * WIDE + s * UNIT
                right_rows[slot, at:at + UNIT, s * LANES:s * LANES + chi] = block[WIDE:]

    def prepare(which):
        slabs, slab, _ = tall.shape
        count = pair * pair
        for leg in range(pair):
            plane = tensor[leg].astype(F32)
            for part in range(slabs):
                lanes = min(LANES, count - part * LANES)
                tall[part, pl.ds(leg, pair, stride=padded), :lanes] = plane[:, part * LANES:part * LANES + lanes]
        for part in range(slabs):
            for other in range(slabs):
                turned[other, part * LANES:(part + 1) * LANES, :] = tall[part, other * LANES:(other + 1) * LANES, :].T
        big, small = order(lax.broadcasted_iota(jnp.int32, (1, count), 1))
        pick_lanes = (lax.broadcasted_iota(jnp.int32, (slab, count), 0) == big * padded + small).astype(F32).astype(BF)
        big, small = order(lax.broadcasted_iota(jnp.int32, (count, 1), 0))

        def finish(source, wanted):
            pick_rows = (lax.broadcasted_iota(jnp.int32, (count, slab), 1) == wanted).astype(F32).astype(BF)
            ordered = jnp.dot(pick_rows, source.astype(BF), preferred_element_type=F32).astype(BF)
            site[which] = jnp.dot(ordered, pick_lanes, preferred_element_type=F32).astype(BF)

        @pl.when(which == 0)
        def _():
            finish(jnp.concatenate([turned[part] for part in range(slabs)], axis=1), big * pair + small)

        @pl.when(which == 1)
        def _():
            for near in range(pair):
                lines = jnp.concatenate([turned[part, pl.ds(near, pair, stride=pair), :] for part in range(slabs)], axis=1)
                for far in range(pair):
                    pieces[far * padded:far * padded + pair, near * padded:(near + 1) * padded] = (
                        lines[:, far * padded:(far + 1) * padded]
                    )
            finish(pieces[...], small * padded + big)

        lay_right(which, lambda lanes: right[which, :, lanes])

    def prepare_left(which):
        for leg in range(pair):
            if leg % 4 == 0:
                left_copy(which, leg // 4).wait_recv()
            block = permuted(leftraw[which, :, leg * chi:(leg + 1) * chi].astype(F32)).T
            for k in range(blocks):
                for s in range(2):
                    piece = block[s * half + k * SUB:s * half + (k + 1) * SUB]
                    if leg < TALL:
                        place = pl.ds(k * block_rows + leg, SUB, stride=TALL)
                    else:
                        place = pl.ds(k * block_rows + tail_at + leg - TALL, SUB, stride=high_legs)
                    left_tall[s, place, :chi] = piece
        for s in range(2):
            left_rows[which, :, s * LANES:(s + 1) * LANES] = left_tall[s].astype(BF)

    def copy_of(which, block, place=None):
        at = pl.multiple_of(block * 2 * SUB, 2 * SUB)
        return pltpu.make_async_remote_copy(
            src_ref=landed.at[FAR, pl.ds(at, 2 * SUB)],
            dst_ref=landed.at[which if place is None else place, pl.ds(at, 2 * SUB)],
            send_sem=send_sem.at[block],
            recv_sem=recv_sem.at[which if place is None else place, block],
            device_id={"row": jnp.where(which == 0, row + 1, row - 1)},
            device_id_type=pl.DeviceIdType.MESH,
        )

    def inverse_norm(square_sum):
        return lax.rsqrt(jnp.full((1, 1), jnp.sum(square_sum) / (chi * pair * chi) + epsilon, F32))

    def unpack(source_at, block):
        at = pl.multiple_of(block * 2 * SUB, 2 * SUB)
        squares = jnp.zeros((SUB, LANES), F32)
        for quad in range(pair // 4):
            tiles = [
                landed[source_at, pl.ds(at, 2 * SUB), (3 * quad + t) * LANES:(3 * quad + t + 1) * LANES]
                for t in range(3)
            ]
            for tile in tiles:
                value = tile.astype(F32)
                squares += jnp.sum((value * value).reshape(2, SUB, LANES), axis=0)

            def unit(leg, part, place):
                source, position = divmod(leg * 3 + part, 4)
                return lane_roll(tiles[source], (place - position) % 4 * UNIT)

            def build(parts, s):
                value = jnp.zeros((TALL, LANES), BF)
                for leg, part, place in parts:
                    value = jnp.where(tall_unit == place, unit(leg, part, place), value)
                return value

            for s in range(2):
                for duo in range(2):
                    base = (2 * quad + duo) * 3 * LANES
                    for v in range(2):
                        leg = 2 * duo + v
                        wide[pl.ds(pl.multiple_of(s * LANES + at, TALL), TALL), base + v * LANES:base + (v + 1) * LANES] = (
                            build([(leg, 0, 2 * s), (leg, 1, 2 * s + 1)], s)
                        )
                    wide[pl.ds(pl.multiple_of(s * LANES + at, TALL), TALL), base + 2 * LANES:base + 3 * LANES] = (
                        build([(2 * duo, 2, s), (2 * duo + 1, 2, 2 + s)], s)
                    )
        return squares

    def mix(tile):
        p, q, x = tile[:, :LANES], tile[:, LANES:2 * LANES], tile[:, 2 * LANES:]
        return (
            jnp.where(sub, p, swap_sub(q)),
            jnp.where(sub, swap_sub(p), q),
            jnp.where(diag, x, swap_lanes(swap_sub(x))),
        )

    def cross(upper, lower):
        x, y = upper[:, 2 * LANES:], lower[:, 2 * LANES:]
        return jnp.where(low_tall, x, swap_lanes(y)), jnp.where(low_tall, swap_lanes(x), y)

    def absorb(which, slot, place, sends, first_group, last_group):
        total[...] = jnp.zeros_like(total)
        split = pair * TALL

        def contract_left(block):
            left_here = left_rows[slot, pl.ds(pl.multiple_of(block * block_rows, block_rows), block_rows), :]
            for quad in range(pair // 4):
                part = jnp.dot(left_here, wide[:, quad * 6 * LANES:(quad + 1) * 6 * LANES], preferred_element_type=F32)
                halves = [part[:, :3 * LANES], part[:, 3 * LANES:]]
                for duo in range(2):
                    at = (2 * quad + duo) * 2 * TALL
                    for two in range(SUB // 2):
                        upper = halves[duo][2 * two * TALL:(2 * two + 1) * TALL]
                        lower = halves[duo][(2 * two + 1) * TALL:(2 * two + 2) * TALL]
                        pairs = (
                            (upper[:, :LANES], upper[:, LANES:2 * LANES]),
                            (lower[:, :LANES], lower[:, LANES:2 * LANES]),
                            cross(upper, lower),
                        )
                        for t in range(3):
                            lanes = slice((3 * two + t) * LANES, (3 * two + t + 1) * LANES)
                            first[at:at + TALL, lanes] = pairs[t][0].astype(BF)
                            first[at + TALL:at + 2 * TALL, lanes] = pairs[t][1].astype(BF)
                for two in range(SUB // 2):
                    mixed = [mix(halves[duo][tail_at + two * SUB:tail_at + (two + 1) * SUB]) for duo in range(2)]
                    for t in range(3):
                        first[split + quad * TALL:split + (quad + 1) * TALL, (3 * two + t) * LANES:(3 * two + t + 1) * LANES] = (
                            jnp.concatenate([mixed[0][t], mixed[1][t]], axis=0).astype(BF)
                        )

        def contract_site():
            for four in range(SUB // 4):
                part = jnp.dot(site[slot], first[:, four * 6 * LANES:(four + 1) * 6 * LANES], preferred_element_type=F32)
                halves = [part[:, :3 * LANES], part[:, 3 * LANES:]]
                for duo in range(pair // 2):
                    for two in range(2):
                        at = (4 * four + 2 * two) * TALL
                        upper = halves[two][2 * duo * TALL:(2 * duo + 1) * TALL]
                        lower = halves[two][(2 * duo + 1) * TALL:(2 * duo + 2) * TALL]
                        pairs = (
                            (upper[:, :LANES], upper[:, LANES:2 * LANES]),
                            (lower[:, :LANES], lower[:, LANES:2 * LANES]),
                            cross(upper, lower),
                        )
                        for t in range(3):
                            lanes = slice((3 * duo + t) * LANES, (3 * duo + t + 1) * LANES)
                            spread[at:at + TALL, lanes] = pairs[t][0].astype(BF)
                            spread[at + TALL:at + 2 * TALL, lanes] = pairs[t][1].astype(BF)
                    mixed = [mix(halves[two][split + duo * SUB:split + (duo + 1) * SUB]) for two in range(2)]
                    for t in range(3):
                        spread[tail_at + four * TALL:tail_at + (four + 1) * TALL, (3 * duo + t) * LANES:(3 * duo + t + 1) * LANES] = (
                            jnp.concatenate([mixed[0][t], mixed[1][t]], axis=0).astype(BF)
                        )

        def contract_right(block):
            done = jnp.dot(spread[...], right_rows[slot], preferred_element_type=F32) * scaling[...]
            total[...] += jnp.sum((done * done).reshape(-1, SUB, 2 * LANES), axis=0)
            for s in range(2):
                out[s] = done[:, s * LANES:(s + 1) * LANES]
            at = pl.multiple_of(block * 2 * SUB, 2 * SUB)
            for quad in range(pair // 4):
                lines = []
                for leg in range(4 * quad, 4 * quad + 4):
                    if leg < TALL:
                        place = pl.ds(leg, SUB, stride=TALL)
                    else:
                        place = pl.ds(tail_at + leg - TALL, SUB, stride=high_legs)
                    lines.append([out[s, place, :] for s in range(2)])
                both = []
                for s in range(2):
                    moved = [
                        lane_roll(lines[leg][s], (-leg) % 4 * UNIT) for leg in range(4)
                    ]
                    both.append([
                        jnp.where(lane_unit < 3 - t, moved[t], moved[t + 1]) for t in range(3)
                    ])
                for t in range(3):
                    lanes = slice((3 * quad + t) * LANES, (3 * quad + t + 1) * LANES)
                    for s in range(2):
                        grown[pl.ds(pl.multiple_of(s * half + block * SUB, SUB), SUB), lanes] = both[s][t]
                    landed[FAR, pl.ds(at, 2 * SUB), lanes] = jnp.concatenate([both[0][t], both[1][t]], axis=0).astype(BF)

        def one_group(group, carry):
            for step in range(GROUP):
                block = group * GROUP + step
                if step == 0:
                    contract_left(block)
                contract_site()
                if step < GROUP - 1:
                    contract_left(block + 1)
                else:
                    @pl.when(sends)
                    def _():
                        for done in range(step):
                            copy_of(which, block - step + done, place).start()
                contract_right(block)

            @pl.when(sends)
            def _():
                copy_of(which, group * GROUP + GROUP - 1, place).start()

            return carry

        lax.fori_loop(first_group, last_group, one_group, 0)

    def collect(which):
        squares = total[:, :LANES] + total[:, LANES:]
        for block in range(blocks // 2, blocks):
            copy_of(which, block).wait_recv()
            for lanes in range(0, pair * chi, LANES):
                values = landed[which, block * 2 * SUB:(block + 1) * 2 * SUB, lanes:lanes + LANES].astype(F32)
                for s in range(2):
                    value = values[s * SUB:(s + 1) * SUB]
                    squares += value * value
                    grown[s * half + block * SUB:s * half + (block + 1) * SUB, lanes:lanes + LANES] = value
        total[:, :LANES] = squares
        total[:, LANES:] = jnp.zeros((SUB, LANES), F32)

    def one_turn(turn, carry):
        last = turn == rows - 1
        owns = (row == turn) | (row == rows - 1 - turn)
        helps = last & helping if split else jnp.bool_(False)
        finishes = last & owns if split else jnp.bool_(False)
        sends = jnp.logical_not(last & owns)
        active = owns | helps
        which = jnp.where(row == jnp.where(helps, rows - 2, turn), 0, 1)
        slot = jnp.where(helps, FAR, which)
        place = jnp.where(helps, 1 - which, which)
        first_group = jnp.where(helps, 1, 0)
        last_group = jnp.where(finishes, 1, groups)
        early = jnp.where((row == 0) | (row == rows - 1), 1, 2)

        def one_prepare(step, carry):
            mine = jnp.where(step == 0, begin, 1 - begin)
            prepare(mine)
            return carry

        def one_prepare_left(step, carry):
            mine = jnp.where(step == 0, begin, 1 - begin)
            prepare_left(mine)
            if split:
                @pl.when(outer & (step == 1))
                def _():
                    far_copy(1).start()
                    far_copy(2).start()

            return carry

        @pl.when(turn == 0)
        def _():
            copy_in(tensor_hbm, tensor, 0).wait()
            copy_in(right_hbm, right, 1).wait()
            copy_in(top_hbm, held, 2).wait()

        @pl.when(active & (turn == 0))
        def _():
            for lanes in range(0, pair * chi, LANES):
                landed[which, :, lanes:lanes + LANES] = permuted(held[:, lanes:lanes + LANES].astype(F32)).astype(BF)

        from_step = jnp.where(turn == 0, 0, jnp.where(turn == 1, early, 2))
        to_step = jnp.where(turn == 0, early, 2)
        lax.fori_loop(from_step, to_step, one_prepare, 0)

        @pl.when(active)
        def _():
            def one_unpack(block, squares):
                @pl.when((turn > 0) & jnp.logical_not(helps))
                def _():
                    copy_of(which, block).wait_recv()

                return squares + unpack(slot, block)

            squares = lax.fori_loop(0, blocks, one_unpack, jnp.zeros((SUB, LANES), F32))
            norm = jnp.where(turn > 0, inverse_norm(squares), jnp.ones((1, 1), F32))
            scaling[...] = jnp.broadcast_to(norm, scaling.shape)

        lax.fori_loop(from_step, to_step, one_prepare_left, 0)

        if split:
            @pl.when(helping & (turn == 0))
            def _():
                far_copy(0).wait_recv()
                lay_right(FAR, lambda lanes: right_far[:, lanes])

        @pl.when(helps)
        def _():
            far_copy(1).wait_recv()
            far_copy(2).wait_recv()

        @pl.when(active & (turn > jnp.minimum(row, rows - 1 - row)))
        def _():
            for block in range(blocks):
                copy_of(which, block).wait_send()

        @pl.when(active)
        def _():
            absorb(which, slot, place, sends, first_group, last_group)

        @pl.when(finishes)
        def _():
            collect(1 - which)

        @pl.when(owns)
        def _():
            env_ref[which] = (grown[...] * inverse_norm(total[...])).astype(BF)

        return carry

    lax.fori_loop(0, rows, one_turn, 0)

    def one_wait(block, carry):
        copy_of(begin, block).wait_send()
        return carry

    lax.fori_loop(jnp.where(outer, blocks, jnp.where(helping, blocks // 2, 0)), blocks, one_wait, 0)
    if split:
        @pl.when(outer)
        def _():
            for item in range(3):
                far_copy(item).wait_send()

    for which in range(2):
        for chunk in range(chunks):
            left_copy(which, chunk).wait_send()


def sweep(rows, cols, top, bottom, tensor, left, right, chi, pair):
    slab = round_up(pair * round_up(pair, SUB), LANES)
    count = pair * pair
    half = chi // 2
    blocks = half // SUB
    lanes = pair // 2 * 3 * LANES
    return pl.pallas_call(
        functools.partial(sweep_kernel, rows, cols, chi, pair),
        out_shape=jax.ShapeDtypeStruct((2,) + top.shape, top.dtype),
        in_specs=[pl.BlockSpec(memory_space=pltpu.HBM)] * 5,
        out_specs=pl.BlockSpec(memory_space=pltpu.VMEM),
        scratch_shapes=[
            pltpu.VMEM(tensor.shape, BF),
            pltpu.VMEM(right.shape, BF),
            pltpu.VMEM(top.shape, BF),
            pltpu.VMEM(left.shape, BF),
            pltpu.VMEM((slab // LANES, slab, LANES), F32),
            pltpu.VMEM((slab // LANES, slab, LANES), F32),
            pltpu.VMEM((slab, slab), F32),
            pltpu.VMEM((3, count, count), BF),
            pltpu.VMEM((2, half * pair, LANES), F32),
            pltpu.VMEM((3, half * pair, 2 * LANES), BF),
            pltpu.VMEM((3, lanes, 2 * LANES), BF),
            pltpu.VMEM((2 * LANES, lanes), BF),
            pltpu.VMEM((count, SUB // 2 * 3 * LANES), BF),
            pltpu.VMEM((SUB * pair, lanes), BF),
            pltpu.VMEM((2, SUB * pair, LANES), F32),
            pltpu.VMEM(top.shape, F32),
            pltpu.VMEM((SUB, 2 * LANES), F32),
            pltpu.VMEM((3,) + top.shape, BF),
            pltpu.VMEM((1, 2 * LANES), F32),
            pltpu.VMEM(top.shape, BF),
            pltpu.SemaphoreType.DMA((3,)),
            pltpu.SemaphoreType.DMA((2, pair // 4)),
            pltpu.SemaphoreType.DMA((2, pair // 4)),
            pltpu.SemaphoreType.DMA((blocks,)),
            pltpu.SemaphoreType.DMA((2, blocks)),
            pltpu.SemaphoreType.DMA((3,)),
            pltpu.SemaphoreType.DMA((3,)),
        ],
        compiler_params=pltpu.CompilerParams(collective_id=0, has_side_effects=True, vmem_limit_bytes=40 * 1024 * 1024),
        name="sweep",
    )(*[pltpu.with_memory_space_constraint(x, pltpu.HBM) for x in (top, bottom, tensor, left, right)])


def local(top_in, bottom_in, row_tensor, left_proj, right_proj):
    chi = top_in.shape[1]
    pair = row_tensor.shape[2]
    env = sweep(
        lax.axis_size("row"), lax.axis_size("col"), top_in[0], bottom_in[0], row_tensor[0, 0],
        left_proj[:, 0, 0], right_proj[:, 0, 0], chi, pair,
    )
    return env[:, None, None]


def solution(mesh):
    return jax.shard_map(
        local,
        mesh=mesh,
        in_specs=(
            P("col", None, None),
            P("col", None, None),
            P("row", "col", None, None, None),
            P(None, "row", "col", None, None),
            P(None, "row", "col", None, None),
        ),
        out_specs=P(None, "row", "col", None, None),
        check_vma=False,
    )
```
